32 devices in a mesh: cells: 8 (over y, x, core), vecs: 4 (over z).
Axes of the slice: x: 2, y: 2, z: 4, core: 2. Of those that a mesh axis runs over, the one named last changes fastest.
Arguments:
- vectors: float32 [64, 8, 64, 128], P(None, 'cells', 'vecs'), may hold values from -120 to 120
- potential: float32 [64, 8, 128], P(None, 'cells'), may hold values from -0.5 to 0.5
- hopping: float32 [27, 64, 64], replicated, may hold values from -0.07 to 0.07
- center: float32 [1], replicated, may hold values from -0.3 to 0.3
Outputs:
- filtered: float32 [64, 8, 64, 128], P(None, 'cells', 'vecs')
The draws below stay inside these ranges and needn't reach their ends.
All inputs are finite; a program needn't handle non-finite values.
Results may differ from the reference program's by a relative error of at most 0.0003.
Values sent between devices are 32-bit elements; how exact they have to be, the bound alone decides.
A program may use at most 128 MiB of HBM per device.

```python
import math
import jax
import jax.numpy as jnp
from jax import lax

ORB = 64
NVEC = 64
NY = 16
STEPS = 4
NX = 8
NZ = 8


def draw_vectors(key, part):
    base_key, spread_key, weight_key = jax.random.split(jax.random.fold_in(key, 11), 3)
    base = jax.random.truncated_normal(base_key, -4.0, 4.0, (ORB, NX, NVEC, NY * NZ), jnp.float32)
    common = 0.5
    spread = jax.random.truncated_normal(spread_key, -4.0, 4.0, (NVEC, NVEC), jnp.float32)
    weights = jax.random.uniform(weight_key, (NVEC,), jnp.float32, -1.0, 1.0)
    scale = 1.0 / math.sqrt(NVEC)
    mixer = jnp.eye(NVEC, dtype=jnp.float32) + 0.7 * scale * spread
    mixer = mixer + common * scale * jnp.ones((NVEC, 1), jnp.float32) * weights[None, :]
    return jnp.einsum('oxkc,ku->oxuc', base, mixer)


def levels(key, shape, cuts, least, largest):
    loudness = 1.0
    for axis_at, parts in cuts:
        steps = jax.random.uniform(jax.random.fold_in(jax.random.fold_in(key, 6), axis_at), (parts,), jnp.float32, least / len(cuts), largest / len(cuts))
        loudness = loudness * jnp.repeat(jnp.exp(steps), shape[axis_at] // parts).reshape((-1,) + (1,) * (len(shape) - 1 - axis_at))
    return loudness


def scatter_about(own_key, dims, deviation, most, held_as=jnp.bfloat16):
    array = deviation * jax.random.normal(own_key, dims, jnp.float32)
    return jnp.clip(array, min=-most, max=most).astype(held_as)


def setup_inputs(seed: int = 0) -> dict:
    key_of = jax.random.split(jax.random.key(seed), 5)
    return {
        "vectors": draw_vectors(jax.random.fold_in(key_of[4], 71), 0),
        "potential": jnp.clip(jax.random.uniform(key_of[1], (ORB, NX, NY * NZ), jnp.float32, -0.5, 0.5) * levels(key_of[1], (ORB, NX, NY * NZ), ((1, 8),), -0.4, 0.0), -0.5, 0.5),
        "hopping": scatter_about(key_of[2], (27, ORB, ORB), 0.012, 0.07, jnp.float32),
        "center": jnp.clip(jax.random.uniform(key_of[3], (1,), jnp.float32, -0.3, 0.3), -0.3, 0.3),
    }


HIGH = lax.Precision.HIGHEST

def symmetric_blocks(hopping):
    return 0.5 * (hopping + jnp.transpose(hopping[::-1], (0, 2, 1)))

def apply_lattice(field_in, potential, center, blocks):
    orbits, width_x, bundle, merged = field_in.shape

    def one_slice(index):
        onsite = lax.dynamic_index_in_dim(potential, index, 1, keepdims=False) - center[0]
        own = lax.dynamic_index_in_dim(field_in, index, 1, keepdims=False)
        running = onsite[:, None, :] * own
        for offset in range(3):
            where = (index + offset - 1 + width_x) % width_x
            source = lax.dynamic_index_in_dim(field_in, where, 1, keepdims=False)
            stacked = blocks[9 * offset:9 * offset + 9].reshape(9 * orbits, orbits)
            product = jnp.dot(stacked, source.reshape(orbits, -1), precision=HIGH, preferred_element_type=jnp.float32)
            product = product.reshape(9, orbits, bundle, NY, NZ)
            for inner in range(9):
                moved = jnp.roll(product[inner], (1 - inner // 3, 1 - inner % 3), axis=(2, 3))
                running = running + moved.reshape(orbits, bundle, merged)
        return running
    slices = lax.map(one_slice, jnp.arange(width_x, dtype=jnp.int32))
    return jnp.moveaxis(slices, 0, 1)

def reference(vectors, potential, hopping, center):
    blocks = symmetric_blocks(hopping)
    previous = vectors
    current = apply_lattice(vectors, potential, center, blocks)
    for step in range(STEPS - 1):
        following = 2.0 * apply_lattice(current, potential, center, blocks) - previous
        previous, current = (current, following)
    gram_matrix = lax.dot_general(current, current, (((0, 1, 3), (0, 1, 3)), ((), ())), precision=HIGH, preferred_element_type=jnp.float32)
    frobenius = jnp.sqrt(jnp.sum(gram_matrix * gram_matrix))
    mixing = (1.5 * jnp.eye(NVEC, dtype=jnp.float32) - 0.5 * gram_matrix / frobenius) / jnp.sqrt(frobenius)
    result = jnp.einsum('oxuc,uv->oxvc', current, mixing, precision=HIGH)
    return result * jnp.sqrt(jnp.float32(NX * NY * NZ))
```

```python
import functools
import math

import jax
import jax.numpy as jnp
from jax import lax
from jax.experimental import pallas as pl
from jax.experimental.pallas import tpu as pltpu
from jax.sharding import PartitionSpec as P

NVEC = 64
NY = 16
STEPS = 4
NZ = 8


HIGH = lax.Precision.HIGHEST


def with_halo(x, sides, width):
    for axis, dim in sides:
        peers, length = (lax.axis_size(axis), x.shape[dim])
        up = [(i, (i + 1) % peers) for i in range(peers)]
        down = [(j, i) for i, j in up]
        last = lax.slice_in_dim(x, length - width, length, axis=dim)
        initial = lax.slice_in_dim(x, 0, width, axis=dim)
        before = lax.ppermute(last, axis, up)
        after = lax.ppermute(initial, axis, down)
        x = jnp.concatenate([before, x, after], axis=dim)
    return x


def symmetric_blocks(hopping):
    return 0.5 * (hopping + jnp.transpose(hopping[::-1], (0, 2, 1)))


def apply_lattice(field_in, potential, center, blocks):
    orbits, width_x, bundle, merged = field_in.shape
    padded = with_halo(field_in, (("cells", 1),), 1)
    grid_view = padded.reshape(orbits, width_x + 2, bundle, NY, NZ)
    running = (potential - center[0])[:, :, None, :] * field_in
    for inner in range(9):
        shift_y = inner // 3 - 1
        shift_z = inner % 3 - 1
        shifted = jnp.roll(grid_view, (-shift_y, -shift_z), axis=(3, 4)).reshape(
            orbits, width_x + 2, bundle, merged
        )
        for offset in range(3):
            source = shifted[:, offset : offset + width_x].reshape(orbits, -1)
            product = jnp.dot(
                blocks[9 * offset + inner],
                source,
                precision=HIGH,
                preferred_element_type=jnp.float32,
            )
            running = running + product.reshape(orbits, width_x, bundle, merged)
    return running


def inner_rows(left, right):
    return lax.dot_general(
        left,
        right,
        (((0, 1, 3), (0, 1, 3)), ((), ())),
        precision=HIGH,
        preferred_element_type=jnp.float32,
    )


def shards(vectors, potential, hopping, center):
    blocks = symmetric_blocks(hopping)
    previous = vectors
    current = apply_lattice(vectors, potential, center, blocks)
    for step in range(STEPS - 1):
        following = 2.0 * apply_lattice(current, potential, center, blocks) - previous
        previous, current = (current, following)
    total_cells = current.shape[1] * lax.axis_size("cells") * current.shape[3]
    factor = math.sqrt(float(total_cells))
    by_cells = lax.all_to_all(current, "vecs", split_axis=3, concat_axis=2, tiled=True)
    gram_matrix = lax.psum(inner_rows(by_cells, by_cells), ("cells", "vecs"))
    frobenius = jnp.sqrt(jnp.sum(gram_matrix * gram_matrix))
    mixing = (1.5 * jnp.eye(NVEC, dtype=jnp.float32) - 0.5 * gram_matrix / frobenius) / jnp.sqrt(
        frobenius
    )
    mixed = jnp.einsum("oxuc,uv->oxvc", by_cells, mixing, precision=HIGH) * factor
    return lax.all_to_all(mixed, "vecs", split_axis=2, concat_axis=3, tiled=True)


def split_pair(value):
    high = value.astype(jnp.bfloat16)
    low = (value - high.astype(jnp.float32)).astype(jnp.bfloat16)
    return high, low


def pack_kernel(dests, center_ref, vectors_ref, potential_ref, out_ref):
    orbits = potential_ref.shape[0]
    bundle = vectors_ref.shape[0] // orbits
    own = bundle // dests
    onsite = potential_ref[:, 0, :] - center_ref[0]
    for n in range(bundle):
        d, t = n // own, n % own
        out_ref[d, t * orbits : (t + 1) * orbits, :] = vectors_ref[pl.ds(n, orbits, stride=bundle), :]
    for d in range(dests):
        out_ref[d, own * orbits :, :] = onsite


def build_weights(hopping_ref, weights):
    orbits = hopping_ref.shape[1]
    for inner in range(9):
        parts = []
        for offset in range(3):
            d = 9 * offset + inner
            parts.append(0.5 * (hopping_ref[d] + hopping_ref[26 - d].T))
        row = jnp.concatenate(parts, axis=1)
        high = row.astype(jnp.bfloat16).astype(jnp.float32)
        low = row - high
        weights[inner * orbits : (inner + 1) * orbits, :] = jnp.concatenate(
            [high, high, low], axis=1
        ).astype(jnp.bfloat16)


def gather_shifts(product, orbits):
    lanes = product.shape[1]
    z = lax.broadcasted_iota(jnp.int32, (orbits, lanes), 1) % NZ

    def part(dy, dz):
        if abs(dy) > 1:
            return 0.0
        at = (3 * (dy + 1) + dz + 1) * orbits
        return product[at : at + orbits]

    def moved(value, shift):
        shift = shift % lanes
        return pltpu.roll(value, shift, 1) if shift else value

    total = part(0, 0) + moved(part(-1, 0), NZ) + moved(part(1, 0), -NZ)
    for k in range(-2, 2):
        chosen = jnp.where(z > 0, part(k, 1), part(k + 1, 1))
        total = total + moved(chosen, -1 - NZ * k)
    for k in range(-1, 3):
        chosen = jnp.where(z < NZ - 1, part(k, -1), part(k - 1, -1))
        total = total + moved(chosen, 1 - NZ * k)
    return total


def filter_kernel(own, peers, packed_ref, hopping_ref, out_ref, weights, fields, highs, lows):
    planes = packed_ref.shape[0]
    orbits = hopping_ref.shape[1]
    lanes = packed_ref.shape[2]
    rows = orbits // peers
    build_weights(hopping_ref, weights)

    def put(slot, x, value):
        high, low = split_pair(value)
        at = (x + 1) * orbits
        if not isinstance(x, int):
            at = pl.multiple_of(at, orbits)
        highs[slot, pl.ds(at, orbits), :] = high
        lows[slot, pl.ds(at, orbits), :] = low

    def wrap(slot):
        for ref in (highs, lows):
            ref[slot, 0:orbits, :] = ref[slot, planes * orbits : (planes + 1) * orbits, :]
            ref[slot, (planes + 1) * orbits :, :] = ref[slot, orbits : 2 * orbits, :]

    for x in range(planes):
        value = jnp.concatenate(
            [packed_ref[x, t * orbits : (t + 1) * orbits, :] for t in range(own)], axis=1
        )
        fields[0, x] = value
        put(0, x, value)
    wrap(0)
    for step in range(STEPS):
        now, later = step % 2, (step + 1) % 2

        def body(x, carry):
            at = pl.ds(pl.multiple_of(x * orbits, orbits), 3 * orbits)
            high, low = highs[now, at, :], lows[now, at, :]
            source = jnp.concatenate([high, low, high], axis=0)
            product = jnp.dot(weights[...], source, preferred_element_type=jnp.float32)
            onsite = packed_ref[x, own * orbits :, :]
            results = []
            for t in range(own):
                span = slice(t * lanes, (t + 1) * lanes)
                applied = gather_shifts(product[:, span], orbits) + onsite * fields[now, x, :, span]
                if step:
                    applied = 2.0 * applied - fields[later, x, :, span]
                results.append(applied)
            if step < STEPS - 1:
                value = jnp.concatenate(results, axis=1)
                fields[later, x] = value
                put(later, x, value)
            else:
                for t in range(own):
                    for p in range(peers):
                        out_ref[p * planes + x, t * rows : (t + 1) * rows, :] = results[t][
                            p * rows : (p + 1) * rows
                        ]
            return carry

        lax.fori_loop(0, planes, body, 0, unroll=2)
        if step < STEPS - 1:
            wrap(later)


def exchange(axis, me, count, slots, send_sems, recv_sems):
    def copy(hop):
        peer = lax.rem(me + hop, count)
        return pltpu.make_async_remote_copy(
            src_ref=slots.at[me],
            dst_ref=slots.at[me],
            send_sem=send_sems.at[hop],
            recv_sem=recv_sems.at[hop],
            device_id={axis: peer},
            device_id_type=pl.DeviceIdType.MESH,
        )

    copies = [copy(hop) for hop in range(1, count)]
    for each in copies:
        each.start()
    for each in copies:
        each.wait()
    total = slots[0]
    for i in range(1, count):
        total = total + slots[i]
    return total


def mix_kernel(cells, peers, factor, field_ref, out_ref, first, second, s1, r1, s2, r2):
    mine, place = lax.axis_index("vecs"), lax.axis_index("cells")
    barrier = pltpu.get_barrier_semaphore()
    for axis, me, count in (("vecs", mine, peers), ("cells", place, cells)):
        for hop in range(1, count):
            pl.semaphore_signal(
                barrier,
                inc=1,
                device_id={axis: lax.rem(me + hop, count)},
                device_id_type=pl.DeviceIdType.MESH,
            )
    rows, vectors = out_ref.shape[1], out_ref.shape[0] * out_ref.shape[2]
    lanes, bundle, half = out_ref.shape[3], out_ref.shape[2], vectors // 2
    field = jnp.concatenate(
        [field_ref[pl.ds(o, vectors, stride=rows), :] for o in range(rows)], axis=1
    )
    gram = lax.dot_general(
        field, field, (((1,), (1,)), ((), ())), precision=HIGH, preferred_element_type=jnp.float32
    )
    pl.semaphore_wait(barrier, peers + cells - 2)
    first[mine] = jnp.concatenate([gram[:half], gram[half:]], axis=1)
    second[place] = exchange("vecs", mine, peers, first, s1, r1)
    total = exchange("cells", place, cells, second, s2, r2)
    gram = jnp.concatenate([total[:, :vectors], total[:, vectors:]], axis=0)
    frobenius = jnp.sqrt(jnp.sum(gram * gram, axis=(0, 1), keepdims=True))
    row = lax.broadcasted_iota(jnp.int32, gram.shape, 0)
    column = lax.broadcasted_iota(jnp.int32, gram.shape, 1)
    unit = jnp.where(row == column, 1.5, 0.0)
    mixing = (unit - 0.5 * gram / frobenius) / jnp.sqrt(frobenius)
    mixed = lax.dot_general(
        mixing, field, (((0,), (0,)), ((), ())), precision=HIGH, preferred_element_type=jnp.float32
    )
    for p in range(peers):
        for o in range(rows):
            out_ref[p, o] = (
                mixed[p * bundle : (p + 1) * bundle, o * lanes : (o + 1) * lanes] * factor
            )


def resident_shards(vectors, potential, hopping, center):
    orbits, _, bundle, lanes = vectors.shape
    cells, peers = lax.axis_size("cells"), lax.axis_size("vecs")
    own, rows, planes = bundle // cells, orbits // peers, cells
    vmem, smem = pl.BlockSpec(memory_space=pltpu.VMEM), pl.BlockSpec(memory_space=pltpu.SMEM)
    f32 = jnp.float32
    packed = pl.pallas_call(
        functools.partial(pack_kernel, cells),
        out_shape=jax.ShapeDtypeStruct((cells, (own + 1) * orbits, lanes), f32),
        in_specs=[smem, vmem, vmem],
        out_specs=vmem,
        name="pack",
    )(center, vectors.reshape(orbits * bundle, lanes), potential)
    packed = lax.all_to_all(packed, "cells", split_axis=0, concat_axis=0, tiled=True)
    padded = (2, (planes + 2) * orbits, own * lanes)
    filtered = pl.pallas_call(
        functools.partial(filter_kernel, own, peers),
        out_shape=jax.ShapeDtypeStruct((peers * planes, own * rows, lanes), f32),
        in_specs=[vmem, vmem],
        out_specs=vmem,
        scratch_shapes=[
            pltpu.VMEM((9 * orbits, 9 * orbits), jnp.bfloat16),
            pltpu.VMEM((2, planes, orbits, own * lanes), f32),
            pltpu.VMEM(padded, jnp.bfloat16),
            pltpu.VMEM(padded, jnp.bfloat16),
        ],
        name="filter",
    )(packed, hopping)
    by_rows = lax.all_to_all(filtered, ("vecs", "cells"), split_axis=0, concat_axis=0, tiled=True)
    count = bundle * peers
    factor = math.sqrt(float(cells * lanes))
    dma = pltpu.SemaphoreType.DMA
    mixed = pl.pallas_call(
        functools.partial(mix_kernel, cells, peers, factor),
        out_shape=jax.ShapeDtypeStruct((peers, rows, bundle, lanes), f32),
        in_specs=[vmem],
        out_specs=vmem,
        scratch_shapes=[
            pltpu.VMEM((peers, count // 2, 2 * count), f32),
            pltpu.VMEM((cells, count // 2, 2 * count), f32),
            dma((peers,)),
            dma((peers,)),
            dma((cells,)),
            dma((cells,)),
        ],
        compiler_params=pltpu.CompilerParams(collective_id=0, has_side_effects=True),
        name="mix",
    )(by_rows.reshape(count * rows, lanes))
    result = lax.all_to_all(mixed, "vecs", split_axis=0, concat_axis=0, tiled=True)
    return result.reshape(orbits, 1, bundle, lanes)


def solution(mesh):
    placed = (P(None, "cells", "vecs", None), P(None, "cells", None), P(), P())

    def body(vectors, potential, hopping, center):
        _, width, bundle, merged = vectors.shape
        fits = (
            width == 1
            and bundle % lax.axis_size("cells") == 0
            and vectors.shape[0] % (8 * lax.axis_size("vecs")) == 0
            and merged == 128
        )
        return (resident_shards if fits else shards)(vectors, potential, hopping, center)

    return jax.shard_map(
        body,
        mesh=mesh,
        in_specs=placed,
        out_specs=P(None, "cells", "vecs", None),
        check_vma=False,
    )
```

```python
import functools
import math

import jax
import jax.numpy as jnp
from jax import lax
from jax.experimental import pallas as pl
from jax.experimental.pallas import tpu as pltpu
from jax.sharding import PartitionSpec as P

NVEC = 64
NY = 16
STEPS = 4
NZ = 8


HIGH = lax.Precision.HIGHEST


def with_halo(x, sides, width):
    for axis, dim in sides:
        peers, length = (lax.axis_size(axis), x.shape[dim])
        up = [(i, (i + 1) % peers) for i in range(peers)]
        down = [(j, i) for i, j in up]
        last = lax.slice_in_dim(x, length - width, length, axis=dim)
        initial = lax.slice_in_dim(x, 0, width, axis=dim)
        before = lax.ppermute(last, axis, up)
        after = lax.ppermute(initial, axis, down)
        x = jnp.concatenate([before, x, after], axis=dim)
    return x


def symmetric_blocks(hopping):
    return 0.5 * (hopping + jnp.transpose(hopping[::-1], (0, 2, 1)))


def apply_lattice(field_in, potential, center, blocks):
    orbits, width_x, bundle, merged = field_in.shape
    padded = with_halo(field_in, (("cells", 1),), 1)
    grid_view = padded.reshape(orbits, width_x + 2, bundle, NY, NZ)
    running = (potential - center[0])[:, :, None, :] * field_in
    for inner in range(9):
        shift_y = inner // 3 - 1
        shift_z = inner % 3 - 1
        shifted = jnp.roll(grid_view, (-shift_y, -shift_z), axis=(3, 4)).reshape(
            orbits, width_x + 2, bundle, merged
        )
        for offset in range(3):
            source = shifted[:, offset : offset + width_x].reshape(orbits, -1)
            product = jnp.dot(
                blocks[9 * offset + inner],
                source,
                precision=HIGH,
                preferred_element_type=jnp.float32,
            )
            running = running + product.reshape(orbits, width_x, bundle, merged)
    return running


def inner_rows(left, right):
    return lax.dot_general(
        left,
        right,
        (((0, 1, 3), (0, 1, 3)), ((), ())),
        precision=HIGH,
        preferred_element_type=jnp.float32,
    )


def shards(vectors, potential, hopping, center):
    blocks = symmetric_blocks(hopping)
    previous = vectors
    current = apply_lattice(vectors, potential, center, blocks)
    for step in range(STEPS - 1):
        following = 2.0 * apply_lattice(current, potential, center, blocks) - previous
        previous, current = (current, following)
    total_cells = current.shape[1] * lax.axis_size("cells") * current.shape[3]
    factor = math.sqrt(float(total_cells))
    by_cells = lax.all_to_all(current, "vecs", split_axis=3, concat_axis=2, tiled=True)
    gram_matrix = lax.psum(inner_rows(by_cells, by_cells), ("cells", "vecs"))
    frobenius = jnp.sqrt(jnp.sum(gram_matrix * gram_matrix))
    mixing = (1.5 * jnp.eye(NVEC, dtype=jnp.float32) - 0.5 * gram_matrix / frobenius) / jnp.sqrt(
        frobenius
    )
    mixed = jnp.einsum("oxuc,uv->oxvc", by_cells, mixing, precision=HIGH) * factor
    return lax.all_to_all(mixed, "vecs", split_axis=2, concat_axis=3, tiled=True)


def split_pair(value):
    high = value.astype(jnp.bfloat16)
    low = (value - high.astype(jnp.float32)).astype(jnp.bfloat16)
    return high, low


def build_weights(hopping_ref, weights):
    orbits = hopping_ref.shape[1]
    for inner in range(9):
        parts = []
        for offset in range(3):
            d = 9 * offset + inner
            parts.append(0.5 * (hopping_ref[d] + hopping_ref[26 - d].T))
        row = jnp.concatenate(parts, axis=1)
        high = row.astype(jnp.bfloat16).astype(jnp.float32)
        low = row - high
        weights[inner * orbits : (inner + 1) * orbits, :] = jnp.concatenate(
            [high, high, low], axis=1
        ).astype(jnp.bfloat16)


def gather_shifts(product, orbits):
    lanes = product.shape[1]
    z = lax.broadcasted_iota(jnp.int32, (orbits, lanes), 1) % NZ

    def part(dy, dz):
        if abs(dy) > 1:
            return 0.0
        at = (3 * (dy + 1) + dz + 1) * orbits
        return product[at : at + orbits]

    def moved(value, shift):
        shift = shift % lanes
        return pltpu.roll(value, shift, 1) if shift else value

    total = part(0, 0) + moved(part(-1, 0), NZ) + moved(part(1, 0), -NZ)
    for k in range(-2, 2):
        chosen = jnp.where(z > 0, part(k, 1), part(k + 1, 1))
        total = total + moved(chosen, -1 - NZ * k)
    for k in range(-1, 3):
        chosen = jnp.where(z < NZ - 1, part(k, -1), part(k - 1, -1))
        total = total + moved(chosen, 1 - NZ * k)
    return total


def remote(source, target, send, receive, device):
    return pltpu.make_async_remote_copy(
        src_ref=source,
        dst_ref=target,
        send_sem=send,
        recv_sem=receive,
        device_id=device,
        device_id_type=pl.DeviceIdType.MESH,
    )


def exchange(axis, me, count, slots, send_sems, recv_sems):
    copies = [
        remote(
            slots.at[me],
            slots.at[me],
            send_sems.at[hop],
            recv_sems.at[hop],
            {axis: lax.rem(me + hop, count)},
        )
        for hop in range(1, count)
    ]
    for each in copies:
        each.start()
    for each in copies:
        each.wait()
    total = slots[0]
    for i in range(1, count):
        total = total + slots[i]
    return total


def whole_kernel(
    cells, peers, factor,
    center_ref, vectors_ref, potential_ref, hopping_ref, out_ref,
    packed, arrived, weights, fields, highs, lows, leaving, by_rows, first, second, mixed,
    s1, r1, s2, r2, s3, r3, s4, r4, s5, r5,
):
    mine, place = lax.axis_index("vecs"), lax.axis_index("cells")
    orbits, lanes = hopping_ref.shape[1], packed.shape[2]
    bundle = vectors_ref.shape[0] // orbits
    own, rows, planes = bundle // cells, orbits // peers, cells
    vectors = bundle * peers
    me = mine * cells + place

    barrier = pltpu.get_barrier_semaphore()
    for hop in range(cells):
        for turn in range(peers):
            if hop or turn:
                pl.semaphore_signal(
                    barrier,
                    inc=1,
                    device_id={
                        "cells": lax.rem(place + hop, cells),
                        "vecs": lax.rem(mine + turn, peers),
                    },
                    device_id_type=pl.DeviceIdType.MESH,
                )

    onsite = potential_ref[:, 0, :] - center_ref[0]
    for n in range(bundle):
        d, t = n // own, n % own
        packed[d, t * orbits : (t + 1) * orbits, :] = vectors_ref[pl.ds(n, orbits, stride=bundle), :]
    for d in range(cells):
        packed[d, own * orbits :, :] = onsite
    pl.semaphore_wait(barrier, cells * peers - 1)
    copies = []
    for hop in range(1, cells):
        peer = lax.rem(place + hop, cells)
        copies.append(
            remote(packed.at[peer], arrived.at[place], s1.at[hop], r1.at[hop], {"cells": peer})
        )
    for each in copies:
        each.start()
    arrived[place] = packed[place]
    build_weights(hopping_ref, weights)
    for each in copies:
        each.wait()

    def put(slot, x, value):
        high, low = split_pair(value)
        at = (x + 1) * orbits
        if not isinstance(x, int):
            at = pl.multiple_of(at, orbits)
        highs[slot, pl.ds(at, orbits), :] = high
        lows[slot, pl.ds(at, orbits), :] = low

    def wrap(slot):
        for ref in (highs, lows):
            ref[slot, 0:orbits, :] = ref[slot, planes * orbits : (planes + 1) * orbits, :]
            ref[slot, (planes + 1) * orbits :, :] = ref[slot, orbits : 2 * orbits, :]

    for x in range(planes):
        value = jnp.concatenate(
            [arrived[x, t * orbits : (t + 1) * orbits, :] for t in range(own)], axis=1
        )
        fields[0, x] = value
        put(0, x, value)
    wrap(0)

    def advance(step, x):
        now, later = step % 2, (step + 1) % 2
        at = pl.ds(pl.multiple_of(x * orbits, orbits), 3 * orbits)
        high, low = highs[now, at, :], lows[now, at, :]
        source = jnp.concatenate([high, low, high], axis=0)
        product = jnp.dot(weights[...], source, preferred_element_type=jnp.float32)
        onsite = arrived[x, own * orbits :, :]
        results = []
        for t in range(own):
            span = slice(t * lanes, (t + 1) * lanes)
            applied = gather_shifts(product[:, span], orbits) + onsite * fields[now, x, :, span]
            if step:
                applied = 2.0 * applied - fields[later, x, :, span]
            results.append(applied)
        return results

    for step in range(STEPS - 1):
        later = (step + 1) % 2

        def body(x, carry):
            value = jnp.concatenate(advance(step, x), axis=1)
            fields[later, x] = value
            put(later, x, value)
            return carry

        lax.fori_loop(0, planes, body, 0, unroll=2)
        wrap(later)

    copies = []
    for hop in list(range(1, planes)) + [0]:
        x = lax.rem(place + hop, planes)
        results = advance(STEPS - 1, x)
        for t in range(own):
            for p in range(peers):
                leaving[hop, p, t * rows : (t + 1) * rows, :] = results[t][p * rows : (p + 1) * rows]
        for turn in range(1, peers) if hop == 0 else range(peers):
            p = lax.rem(mine + turn, peers)
            sem = hop * peers + turn
            copy = remote(
                leaving.at[hop, p], by_rows.at[me], s2.at[sem], r2.at[sem], {"cells": x, "vecs": p}
            )
            copy.start()
            copies.append(copy)
    by_rows[me] = leaving[0, mine]
    for each in copies:
        each.wait()

    flat = by_rows.reshape(vectors * rows, lanes)
    field = jnp.concatenate(
        [flat[pl.ds(o, vectors, stride=rows), :] for o in range(rows)], axis=1
    )
    high, low = split_pair(field)
    both = lax.dot_general(
        jnp.concatenate([high, low], axis=0),
        high,
        (((1,), (1,)), ((), ())),
        preferred_element_type=jnp.float32,
    )
    cross = both[vectors:]
    gram = both[:vectors] + cross + cross.T
    half = vectors // 2
    first[mine] = jnp.concatenate([gram[:half], gram[half:]], axis=1)
    second[place] = exchange("vecs", mine, peers, first, s3, r3)
    total = exchange("cells", place, cells, second, s4, r4)
    gram = jnp.concatenate([total[:, :vectors], total[:, vectors:]], axis=0)
    frobenius = jnp.sqrt(jnp.sum(gram * gram, axis=(0, 1), keepdims=True))
    row = lax.broadcasted_iota(jnp.int32, gram.shape, 0)
    column = lax.broadcasted_iota(jnp.int32, gram.shape, 1)
    unit = jnp.where(row == column, 1.5, 0.0)
    mixing = (unit - 0.5 * gram / frobenius) / jnp.sqrt(frobenius)
    mixing_high, mixing_low = split_pair(mixing.T)
    result = factor * jnp.dot(
        jnp.concatenate([mixing_high, mixing_high, mixing_low], axis=1),
        jnp.concatenate([high, low, high], axis=0),
        preferred_element_type=jnp.float32,
    )
    for p in range(peers):
        for o in range(rows):
            mixed[p, o] = result[p * bundle : (p + 1) * bundle, o * lanes : (o + 1) * lanes]
    copies = []
    for turn in range(1, peers):
        p = lax.rem(mine + turn, peers)
        copies.append(remote(mixed.at[p], out_ref.at[mine], s5.at[turn], r5.at[turn], {"vecs": p}))
    for each in copies:
        each.start()
    out_ref[mine] = mixed[mine]
    for each in copies:
        each.wait()


def resident_shards(vectors, potential, hopping, center):
    orbits, _, bundle, lanes = vectors.shape
    cells, peers = lax.axis_size("cells"), lax.axis_size("vecs")
    own, rows, planes = bundle // cells, orbits // peers, cells
    count = bundle * peers
    vmem, smem = pl.BlockSpec(memory_space=pltpu.VMEM), pl.BlockSpec(memory_space=pltpu.SMEM)
    f32, bf16, dma = jnp.float32, jnp.bfloat16, pltpu.SemaphoreType.DMA
    sizes = [n for n in (cells, cells * peers, peers, cells, peers) for _ in range(2)]
    result = pl.pallas_call(
        functools.partial(whole_kernel, cells, peers, math.sqrt(float(cells * lanes))),
        out_shape=jax.ShapeDtypeStruct((peers, rows, bundle, lanes), f32),
        in_specs=[smem, vmem, vmem, vmem],
        out_specs=vmem,
        scratch_shapes=[
            pltpu.VMEM((cells, (own + 1) * orbits, lanes), f32),
            pltpu.VMEM((cells, (own + 1) * orbits, lanes), f32),
            pltpu.VMEM((9 * orbits, 9 * orbits), bf16),
            pltpu.VMEM((2, planes, orbits, own * lanes), f32),
            pltpu.VMEM((2, (planes + 2) * orbits, own * lanes), bf16),
            pltpu.VMEM((2, (planes + 2) * orbits, own * lanes), bf16),
            pltpu.VMEM((planes, peers, own * rows, lanes), f32),
            pltpu.VMEM((peers * planes, own * rows, lanes), f32),
            pltpu.VMEM((peers, count // 2, 2 * count), f32),
            pltpu.VMEM((cells, count // 2, 2 * count), f32),
            pltpu.VMEM((peers, rows, bundle, lanes), f32),
        ]
        + [dma((n,)) for n in sizes],
        compiler_params=pltpu.CompilerParams(
            collective_id=0, has_side_effects=True, vmem_limit_bytes=48 * 1024 * 1024
        ),
        name="whole",
    )(center, vectors.reshape(orbits * bundle, lanes), potential, hopping)
    return result.reshape(orbits, 1, bundle, lanes)


def solution(mesh):
    placed = (P(None, "cells", "vecs", None), P(None, "cells", None), P(), P())

    def body(vectors, potential, hopping, center):
        _, width, bundle, merged = vectors.shape
        fits = (
            width == 1
            and bundle % lax.axis_size("cells") == 0
            and vectors.shape[0] % (8 * lax.axis_size("vecs")) == 0
            and merged == 128
        )
        return (resident_shards if fits else shards)(vectors, potential, hopping, center)

    return jax.shard_map(
        body,
        mesh=mesh,
        in_specs=placed,
        out_specs=P(None, "cells", "vecs", None),
        check_vma=False,
    )
```

```python
import functools
import math

import jax
import jax.numpy as jnp
from jax import lax
from jax.experimental import pallas as pl
from jax.experimental.pallas import tpu as pltpu
from jax.sharding import PartitionSpec as P

NVEC = 64
NY = 16
STEPS = 4
NZ = 8


HIGH = lax.Precision.HIGHEST


def with_halo(x, sides, width):
    for axis, dim in sides:
        peers, length = (lax.axis_size(axis), x.shape[dim])
        up = [(i, (i + 1) % peers) for i in range(peers)]
        down = [(j, i) for i, j in up]
        last = lax.slice_in_dim(x, length - width, length, axis=dim)
        initial = lax.slice_in_dim(x, 0, width, axis=dim)
        before = lax.ppermute(last, axis, up)
        after = lax.ppermute(initial, axis, down)
        x = jnp.concatenate([before, x, after], axis=dim)
    return x


def symmetric_blocks(hopping):
    return 0.5 * (hopping + jnp.transpose(hopping[::-1], (0, 2, 1)))


def apply_lattice(field_in, potential, center, blocks):
    orbits, width_x, bundle, merged = field_in.shape
    padded = with_halo(field_in, (("cells", 1),), 1)
    grid_view = padded.reshape(orbits, width_x + 2, bundle, NY, NZ)
    running = (potential - center[0])[:, :, None, :] * field_in
    for inner in range(9):
        shift_y = inner // 3 - 1
        shift_z = inner % 3 - 1
        shifted = jnp.roll(grid_view, (-shift_y, -shift_z), axis=(3, 4)).reshape(
            orbits, width_x + 2, bundle, merged
        )
        for offset in range(3):
            source = shifted[:, offset : offset + width_x].reshape(orbits, -1)
            product = jnp.dot(
                blocks[9 * offset + inner],
                source,
                precision=HIGH,
                preferred_element_type=jnp.float32,
            )
            running = running + product.reshape(orbits, width_x, bundle, merged)
    return running


def inner_rows(left, right):
    return lax.dot_general(
        left,
        right,
        (((0, 1, 3), (0, 1, 3)), ((), ())),
        precision=HIGH,
        preferred_element_type=jnp.float32,
    )


def shards(vectors, potential, hopping, center):
    blocks = symmetric_blocks(hopping)
    previous = vectors
    current = apply_lattice(vectors, potential, center, blocks)
    for step in range(STEPS - 1):
        following = 2.0 * apply_lattice(current, potential, center, blocks) - previous
        previous, current = (current, following)
    total_cells = current.shape[1] * lax.axis_size("cells") * current.shape[3]
    factor = math.sqrt(float(total_cells))
    by_cells = lax.all_to_all(current, "vecs", split_axis=3, concat_axis=2, tiled=True)
    gram_matrix = lax.psum(inner_rows(by_cells, by_cells), ("cells", "vecs"))
    frobenius = jnp.sqrt(jnp.sum(gram_matrix * gram_matrix))
    mixing = (1.5 * jnp.eye(NVEC, dtype=jnp.float32) - 0.5 * gram_matrix / frobenius) / jnp.sqrt(
        frobenius
    )
    mixed = jnp.einsum("oxuc,uv->oxvc", by_cells, mixing, precision=HIGH) * factor
    return lax.all_to_all(mixed, "vecs", split_axis=2, concat_axis=3, tiled=True)


def split_pair(value):
    high = value.astype(jnp.bfloat16)
    low = (value - high.astype(jnp.float32)).astype(jnp.bfloat16)
    return high, low


def build_weights(hopping_ref, weights):
    orbits = hopping_ref.shape[1]
    for inner in range(9):
        parts = []
        for offset in range(3):
            d = 9 * offset + inner
            parts.append(0.5 * (hopping_ref[d] + hopping_ref[26 - d].T))
        row = jnp.concatenate(parts, axis=1)
        high = row.astype(jnp.bfloat16).astype(jnp.float32)
        low = row - high
        weights[inner * orbits : (inner + 1) * orbits, :] = jnp.concatenate(
            [high, high, low], axis=1
        ).astype(jnp.bfloat16)


def gather_shifts(product, orbits):
    lanes = product.shape[1]
    z = lax.broadcasted_iota(jnp.int32, (orbits, lanes), 1) % NZ

    def part(dy, dz):
        if abs(dy) > 1:
            return 0.0
        at = (3 * (dy + 1) + dz + 1) * orbits
        return product[at : at + orbits]

    def moved(value, shift):
        shift = shift % lanes
        return pltpu.roll(value, shift, 1) if shift else value

    total = part(0, 0) + moved(part(-1, 0), NZ) + moved(part(1, 0), -NZ)
    for k in range(-2, 2):
        chosen = jnp.where(z > 0, part(k, 1), part(k + 1, 1))
        total = total + moved(chosen, -1 - NZ * k)
    for k in range(-1, 3):
        chosen = jnp.where(z < NZ - 1, part(k, -1), part(k - 1, -1))
        total = total + moved(chosen, 1 - NZ * k)
    return total


def remote(source, target, send, receive, device):
    return pltpu.make_async_remote_copy(
        src_ref=source,
        dst_ref=target,
        send_sem=send,
        recv_sem=receive,
        device_id=device,
        device_id_type=pl.DeviceIdType.MESH,
    )


def exchange(axis, me, count, slots, send_sems, recv_sems):
    copies = [
        remote(
            slots.at[me],
            slots.at[me],
            send_sems.at[hop],
            recv_sems.at[hop],
            {axis: lax.rem(me + hop, count)},
        )
        for hop in range(1, count)
    ]
    for each in copies:
        each.start()
    for each in copies:
        each.wait()
    total = slots[0]
    for i in range(1, count):
        total = total + slots[i]
    return total


def demand_order(planes):
    order, known = [], {(0, x) for x in range(planes)}

    def need(step, x):
        if (step, x) in known:
            return
        for near in (-1, 0, 1):
            need(step - 1, (x + near) % planes)
        known.add((step, x))
        order.append((step, x))

    for x in list(range(1, planes)) + [0]:
        need(STEPS, x)
    return order


def whole_kernel(
    cells, peers, factor,
    center_ref, vectors_any, potential_any, hopping_any, out_ref,
    vectors_ref, potential_ref, hopping_ref,
    packed, onsite_ref, planes_in, onsite_in, weights, fields, highs, lows, leaving, by_rows,
    first, second, mixed,
    local, s1, r1, s6, r6, s2, r2, s3, r3, s4, r4, s5, r5,
):
    mine, place = lax.axis_index("vecs"), lax.axis_index("cells")
    orbits, lanes = hopping_ref.shape[1], packed.shape[2]
    bundle = vectors_ref.shape[0] // orbits
    own, rows, planes = bundle // cells, orbits // peers, cells
    vectors = bundle * peers
    me = mine * cells + place

    loads = [
        pltpu.make_async_copy(source, target, local.at[n])
        for n, (source, target) in enumerate(
            (
                (vectors_any, vectors_ref),
                (potential_any, potential_ref),
                (hopping_any, hopping_ref),
            )
        )
    ]
    for each in loads:
        each.start()
    barrier = pltpu.get_barrier_semaphore()
    for hop in range(cells):
        for turn in range(peers):
            if hop or turn:
                pl.semaphore_signal(
                    barrier,
                    inc=1,
                    device_id={
                        "cells": lax.rem(place + hop, cells),
                        "vecs": lax.rem(mine + turn, peers),
                    },
                    device_id_type=pl.DeviceIdType.MESH,
                )

    loads[0].wait()
    for n in range(bundle):
        d, t = n // own, n % own
        packed[d, t * orbits : (t + 1) * orbits, :] = vectors_ref[pl.ds(n, orbits, stride=bundle), :]
    loads[1].wait()
    onsite = potential_ref[:, 0, :] - center_ref[0]
    onsite_ref[...] = onsite
    onsite_in[0] = onsite

    order = demand_order(planes)
    sequence = []
    for step, x in order:
        if step == 1:
            wanted = [("plane", (x + near) % planes) for near in (-1, 0, 1)] + [("onsite", x)]
            sequence += [item for item in wanted if item[1] and item not in sequence]
    arriving = {}
    pl.semaphore_wait(barrier, cells * peers - 1)
    for kind, slot in sequence:
        hop = planes - slot
        peer = lax.rem(place + hop, cells)
        if kind == "plane":
            copy = remote(
                packed.at[peer], planes_in.at[slot], s1.at[hop], r1.at[hop], {"cells": peer}
            )
        else:
            copy = remote(onsite_ref, onsite_in.at[slot], s6.at[hop], r6.at[hop], {"cells": peer})
        copy.start()
        arriving[kind, slot] = copy
    sent = list(arriving.values())
    loads[2].wait()
    build_weights(hopping_ref, weights)

    def put(slot, x, value):
        fields[slot, x] = value
        high, low = split_pair(value)
        highs[slot, x], lows[slot, x] = high, low

    ready = set()

    def receive(x):
        if x in ready:
            return
        ready.add(x)
        if x:
            arriving["plane", x].wait_recv()
            pieces = [planes_in[x, t * orbits : (t + 1) * orbits, :] for t in range(own)]
        else:
            pieces = [packed[place, t * orbits : (t + 1) * orbits, :] for t in range(own)]
        put(0, x, jnp.concatenate(pieces, axis=1))

    def advance(step, x):
        now, later = (step - 1) % 2, step % 2
        around = [(x + near) % planes for near in (-1, 0, 1)]
        high, low = [highs[now, r] for r in around], [lows[now, r] for r in around]
        source = jnp.concatenate(high + low + high, axis=0)
        product = jnp.dot(weights[...], source, preferred_element_type=jnp.float32)
        onsite = onsite_in[x]
        results = []
        for t in range(own):
            span = slice(t * lanes, (t + 1) * lanes)
            applied = gather_shifts(product[:, span], orbits) + onsite * fields[now, x, :, span]
            if step > 1:
                applied = 2.0 * applied - fields[later, x, :, span]
            results.append(applied)
        return results

    copies = []
    for step, x in order:
        if step == 1:
            for near in (-1, 0, 1):
                receive((x + near) % planes)
            if x:
                arriving["onsite", x].wait_recv()
        results = advance(step, x)
        if step < STEPS:
            put(step % 2, x, jnp.concatenate(results, axis=1))
            continue
        for t in range(own):
            for p in range(peers):
                leaving[x, p, t * rows : (t + 1) * rows, :] = results[t][p * rows : (p + 1) * rows]
        for turn in range(1, peers) if x == 0 else range(peers):
            p = lax.rem(mine + turn, peers)
            sem = x * peers + turn
            copy = remote(
                leaving.at[x, p],
                by_rows.at[me],
                s2.at[sem],
                r2.at[sem],
                {"cells": lax.rem(place + x, cells), "vecs": p},
            )
            copy.start()
            copies.append(copy)
    by_rows[me] = leaving[0, mine]
    for each in sent:
        each.wait_send()
    for each in copies:
        each.wait()

    flat = by_rows.reshape(vectors * rows, lanes)
    field = jnp.concatenate(
        [flat[pl.ds(o, vectors, stride=rows), :] for o in range(rows)], axis=1
    )
    high, low = split_pair(field)
    both = lax.dot_general(
        jnp.concatenate([high, low], axis=0),
        high,
        (((1,), (1,)), ((), ())),
        preferred_element_type=jnp.float32,
    )
    cross = both[vectors:]
    gram = both[:vectors] + cross + cross.T
    half = vectors // 2
    first[mine] = jnp.concatenate([gram[:half], gram[half:]], axis=1)
    second[place] = exchange("vecs", mine, peers, first, s3, r3)
    total = exchange("cells", place, cells, second, s4, r4)
    gram = jnp.concatenate([total[:, :vectors], total[:, vectors:]], axis=0)
    frobenius = jnp.sqrt(jnp.sum(gram * gram, axis=(0, 1), keepdims=True))
    row = lax.broadcasted_iota(jnp.int32, gram.shape, 0)
    column = lax.broadcasted_iota(jnp.int32, gram.shape, 1)
    unit = jnp.where(row == column, 1.5, 0.0)
    mixing = (unit - 0.5 * gram / frobenius) / jnp.sqrt(frobenius)
    mixing_high, mixing_low = split_pair(mixing.T)
    result = factor * jnp.dot(
        jnp.concatenate([mixing_high, mixing_high, mixing_low], axis=1),
        jnp.concatenate([high, low, high], axis=0),
        preferred_element_type=jnp.float32,
    )
    for p in range(peers):
        for o in range(rows):
            mixed[p, o] = result[p * bundle : (p + 1) * bundle, o * lanes : (o + 1) * lanes]
    copies = []
    for turn in range(1, peers):
        p = lax.rem(mine + turn, peers)
        copies.append(remote(mixed.at[p], out_ref.at[mine], s5.at[turn], r5.at[turn], {"vecs": p}))
    for each in copies:
        each.start()
    out_ref[mine] = mixed[mine]
    for each in copies:
        each.wait()


def resident_shards(vectors, potential, hopping, center):
    orbits, _, bundle, lanes = vectors.shape
    cells, peers = lax.axis_size("cells"), lax.axis_size("vecs")
    own, rows, planes = bundle // cells, orbits // peers, cells
    count = bundle * peers
    vmem, smem = pl.BlockSpec(memory_space=pltpu.VMEM), pl.BlockSpec(memory_space=pltpu.SMEM)
    held = pl.BlockSpec(memory_space=pl.ANY)
    f32, bf16, dma = jnp.float32, jnp.bfloat16, pltpu.SemaphoreType.DMA
    sizes = [n for n in (cells, cells, cells * peers, peers, cells, peers) for _ in range(2)]
    result = pl.pallas_call(
        functools.partial(whole_kernel, cells, peers, math.sqrt(float(cells * lanes))),
        out_shape=jax.ShapeDtypeStruct((peers, rows, bundle, lanes), f32),
        in_specs=[smem, held, held, held],
        out_specs=vmem,
        scratch_shapes=[
            pltpu.VMEM((orbits * bundle, lanes), f32),
            pltpu.VMEM(potential.shape, f32),
            pltpu.VMEM(hopping.shape, f32),
            pltpu.VMEM((cells, own * orbits, lanes), f32),
            pltpu.VMEM((orbits, lanes), f32),
            pltpu.VMEM((cells, own * orbits, lanes), f32),
            pltpu.VMEM((cells, orbits, lanes), f32),
            pltpu.VMEM((9 * orbits, 9 * orbits), bf16),
            pltpu.VMEM((2, planes, orbits, own * lanes), f32),
            pltpu.VMEM((2, planes, orbits, own * lanes), bf16),
            pltpu.VMEM((2, planes, orbits, own * lanes), bf16),
            pltpu.VMEM((planes, peers, own * rows, lanes), f32),
            pltpu.VMEM((peers * planes, own * rows, lanes), f32),
            pltpu.VMEM((peers, count // 2, 2 * count), f32),
            pltpu.VMEM((cells, count // 2, 2 * count), f32),
            pltpu.VMEM((peers, rows, bundle, lanes), f32),
        ]
        + [dma((3,))]
        + [dma((n,)) for n in sizes],
        compiler_params=pltpu.CompilerParams(
            collective_id=0, has_side_effects=True, vmem_limit_bytes=62 * 1024 * 1024
        ),
        name="whole",
    )(center, vectors.reshape(orbits * bundle, lanes), potential, hopping)
    return result.reshape(orbits, 1, bundle, lanes)


def solution(mesh):
    placed = (P(None, "cells", "vecs", None), P(None, "cells", None), P(), P())

    def body(vectors, potential, hopping, center):
        _, width, bundle, merged = vectors.shape
        fits = (
            width == 1
            and bundle % lax.axis_size("cells") == 0
            and vectors.shape[0] % (8 * lax.axis_size("vecs")) == 0
            and merged == 128
        )
        return (resident_shards if fits else shards)(vectors, potential, hopping, center)

    return jax.shard_map(
        body,
        mesh=mesh,
        in_specs=placed,
        out_specs=P(None, "cells", "vecs", None),
        check_vma=False,
    )
```

```python
import functools
import math

import jax
import jax.numpy as jnp
from jax import lax
from jax.experimental import pallas as pl
from jax.experimental.pallas import tpu as pltpu
from jax.sharding import PartitionSpec as P

NVEC = 64
NY = 16
STEPS = 4
NZ = 8


HIGH = lax.Precision.HIGHEST


def with_halo(x, sides, width):
    for axis, dim in sides:
        peers, length = (lax.axis_size(axis), x.shape[dim])
        up = [(i, (i + 1) % peers) for i in range(peers)]
        down = [(j, i) for i, j in up]
        last = lax.slice_in_dim(x, length - width, length, axis=dim)
        initial = lax.slice_in_dim(x, 0, width, axis=dim)
        before = lax.ppermute(last, axis, up)
        after = lax.ppermute(initial, axis, down)
        x = jnp.concatenate([before, x, after], axis=dim)
    return x


def symmetric_blocks(hopping):
    return 0.5 * (hopping + jnp.transpose(hopping[::-1], (0, 2, 1)))


def apply_lattice(field_in, potential, center, blocks):
    orbits, width_x, bundle, merged = field_in.shape
    padded = with_halo(field_in, (("cells", 1),), 1)
    grid_view = padded.reshape(orbits, width_x + 2, bundle, NY, NZ)
    running = (potential - center[0])[:, :, None, :] * field_in
    for inner in range(9):
        shift_y = inner // 3 - 1
        shift_z = inner % 3 - 1
        shifted = jnp.roll(grid_view, (-shift_y, -shift_z), axis=(3, 4)).reshape(
            orbits, width_x + 2, bundle, merged
        )
        for offset in range(3):
            source = shifted[:, offset : offset + width_x].reshape(orbits, -1)
            product = jnp.dot(
                blocks[9 * offset + inner],
                source,
                precision=HIGH,
                preferred_element_type=jnp.float32,
            )
            running = running + product.reshape(orbits, width_x, bundle, merged)
    return running


def inner_rows(left, right):
    return lax.dot_general(
        left,
        right,
        (((0, 1, 3), (0, 1, 3)), ((), ())),
        precision=HIGH,
        preferred_element_type=jnp.float32,
    )


def shards(vectors, potential, hopping, center):
    blocks = symmetric_blocks(hopping)
    previous = vectors
    current = apply_lattice(vectors, potential, center, blocks)
    for step in range(STEPS - 1):
        following = 2.0 * apply_lattice(current, potential, center, blocks) - previous
        previous, current = (current, following)
    total_cells = current.shape[1] * lax.axis_size("cells") * current.shape[3]
    factor = math.sqrt(float(total_cells))
    by_cells = lax.all_to_all(current, "vecs", split_axis=3, concat_axis=2, tiled=True)
    gram_matrix = lax.psum(inner_rows(by_cells, by_cells), ("cells", "vecs"))
    frobenius = jnp.sqrt(jnp.sum(gram_matrix * gram_matrix))
    mixing = (1.5 * jnp.eye(NVEC, dtype=jnp.float32) - 0.5 * gram_matrix / frobenius) / jnp.sqrt(
        frobenius
    )
    mixed = jnp.einsum("oxuc,uv->oxvc", by_cells, mixing, precision=HIGH) * factor
    return lax.all_to_all(mixed, "vecs", split_axis=2, concat_axis=3, tiled=True)


def split_pair(value):
    high = value.astype(jnp.bfloat16)
    low = (value - high.astype(jnp.float32)).astype(jnp.bfloat16)
    return high, low


def build_weights(hopping_ref, weights):
    orbits = hopping_ref.shape[1]
    for inner in range(9):
        parts = []
        for offset in range(3):
            d = 9 * offset + inner
            parts.append(0.5 * (hopping_ref[d] + hopping_ref[26 - d].T))
        row = jnp.concatenate(parts, axis=1)
        high = row.astype(jnp.bfloat16).astype(jnp.float32)
        low = row - high
        weights[inner * orbits : (inner + 1) * orbits, :] = jnp.concatenate(
            [high, high, low], axis=1
        ).astype(jnp.bfloat16)


def gather_shifts(product, orbits):
    lanes = product.shape[1]
    z = lax.broadcasted_iota(jnp.int32, (orbits, lanes), 1) % NZ

    def part(dy, dz):
        if abs(dy) > 1:
            return 0.0
        at = (3 * (dy + 1) + dz + 1) * orbits
        return product[at : at + orbits]

    def moved(value, shift):
        shift = shift % lanes
        return pltpu.roll(value, shift, 1) if shift else value

    total = part(0, 0) + moved(part(-1, 0), NZ) + moved(part(1, 0), -NZ)
    for k in range(-2, 2):
        chosen = jnp.where(z > 0, part(k, 1), part(k + 1, 1))
        total = total + moved(chosen, -1 - NZ * k)
    for k in range(-1, 3):
        chosen = jnp.where(z < NZ - 1, part(k, -1), part(k - 1, -1))
        total = total + moved(chosen, 1 - NZ * k)
    return total


def remote(source, target, send, receive, device):
    return pltpu.make_async_remote_copy(
        src_ref=source,
        dst_ref=target,
        send_sem=send,
        recv_sem=receive,
        device_id=device,
        device_id_type=pl.DeviceIdType.MESH,
    )


def exchange(axis, me, count, slots, send_sems, recv_sems):
    copies = [
        remote(
            slots.at[me],
            slots.at[me],
            send_sems.at[hop],
            recv_sems.at[hop],
            {axis: lax.rem(me + hop, count)},
        )
        for hop in range(1, count)
    ]
    for each in copies:
        each.start()
    for each in copies:
        each.wait()
    total = slots[0]
    for i in range(1, count):
        total = total + slots[i]
    return total


def demand_order(planes):
    order, known = [], {(1, x) for x in range(planes)}

    def need(step, x):
        if (step, x) in known:
            return
        for near in (-1, 0, 1):
            need(step - 1, (x + near) % planes)
        known.add((step, x))
        order.append((step, x))

    for x in list(range(1, planes)) + [0]:
        need(STEPS, x)
    return order


def whole_kernel(
    cells, peers, factor,
    center_ref, vectors_any, potential_any, hopping_any, out_ref,
    vectors_ref, potential_ref, hopping_ref,
    packed, onsite_ref, planes_in, onsite_in, weights, fields, highs, lows, leaving, by_rows,
    first, second, mixed,
    local, s1, r1, s6, r6, s2, r2, s3, r3, s4, r4, s5, r5,
):
    mine, place = lax.axis_index("vecs"), lax.axis_index("cells")
    orbits, lanes = hopping_ref.shape[1], packed.shape[2]
    bundle = vectors_ref.shape[0] // orbits
    own, rows, planes = bundle // cells, orbits // peers, cells
    vectors = bundle * peers
    me = mine * cells + place

    loads = [
        pltpu.make_async_copy(source, target, local.at[n])
        for n, (source, target) in enumerate(
            (
                (vectors_any, vectors_ref),
                (potential_any, potential_ref),
                (hopping_any, hopping_ref),
            )
        )
    ]
    for each in loads:
        each.start()
    barrier = pltpu.get_barrier_semaphore()
    for hop in range(cells):
        for turn in range(peers):
            if hop or turn:
                pl.semaphore_signal(
                    barrier,
                    inc=1,
                    device_id={
                        "cells": lax.rem(place + hop, cells),
                        "vecs": lax.rem(mine + turn, peers),
                    },
                    device_id_type=pl.DeviceIdType.MESH,
                )

    loads[0].wait()
    for n in range(bundle):
        d, t = n // own, n % own
        packed[d, t * orbits : (t + 1) * orbits, :] = vectors_ref[pl.ds(n, orbits, stride=bundle), :]
    loads[1].wait()
    onsite = potential_ref[:, 0, :] - center_ref[0]
    onsite_ref[...] = onsite
    onsite_in[0] = onsite

    pl.semaphore_wait(barrier, cells * peers - 1)
    plane_copies, onsite_copies = [], []
    for hop in range(1, cells):
        peer, slot = lax.rem(place + hop, cells), cells - hop
        plane_copies.append(
            remote(packed.at[peer], planes_in.at[slot], s1.at[hop], r1.at[hop], {"cells": peer})
        )
        onsite_copies.append(
            remote(onsite_ref, onsite_in.at[slot], s6.at[hop], r6.at[hop], {"cells": peer})
        )
    for each in plane_copies + onsite_copies:
        each.start()
    loads[2].wait()
    build_weights(hopping_ref, weights)
    for each in plane_copies:
        each.wait()

    def put(slot, x, value):
        fields[slot, x] = value
        high, low = split_pair(value)
        highs[slot, x], lows[slot, x] = high, low

    for x in range(planes):
        held = packed.at[place] if x == 0 else planes_in.at[x]
        put(0, x, jnp.concatenate([held[t * orbits : (t + 1) * orbits, :] for t in range(own)], axis=1))

    def advance(step, x):
        now, later = (step - 1) % 2, step % 2
        around = [(x + near) % planes for near in (-1, 0, 1)]
        high, low = [highs[now, r] for r in around], [lows[now, r] for r in around]
        source = jnp.concatenate(high + low + high, axis=0)
        product = jnp.dot(weights[...], source, preferred_element_type=jnp.float32)
        moved = [gather_shifts(product[:, t * lanes : (t + 1) * lanes], orbits) for t in range(own)]
        if step == 1:
            return moved
        return [
            2.0 * (each + onsite_in[x] * fields[now, x, :, span]) - fields[later, x, :, span]
            for each, span in zip(moved, spans)
        ]

    spans = [slice(t * lanes, (t + 1) * lanes) for t in range(own)]
    for x in range(planes):
        fields[1, x] = jnp.concatenate(advance(1, x), axis=1)
    for each in onsite_copies:
        each.wait()
    for x in range(planes):
        onsite = jnp.concatenate([onsite_in[x]] * own, axis=1)
        put(1, x, fields[1, x] + onsite * fields[0, x])

    copies = []
    for step, x in demand_order(planes):
        results = advance(step, x)
        if step < STEPS:
            put(step % 2, x, jnp.concatenate(results, axis=1))
            continue
        for t in range(own):
            for p in range(peers):
                leaving[x, p, t * rows : (t + 1) * rows, :] = results[t][p * rows : (p + 1) * rows]
        for turn in range(1, peers) if x == 0 else range(peers):
            p = lax.rem(mine + turn, peers)
            sem = x * peers + turn
            copy = remote(
                leaving.at[x, p],
                by_rows.at[me],
                s2.at[sem],
                r2.at[sem],
                {"cells": lax.rem(place + x, cells), "vecs": p},
            )
            copy.start()
            copies.append(copy)
    by_rows[me] = leaving[0, mine]
    for each in copies:
        each.wait()

    flat = by_rows.reshape(vectors * rows, lanes)
    field = jnp.concatenate(
        [flat[pl.ds(o, vectors, stride=rows), :] for o in range(rows)], axis=1
    )
    high, low = split_pair(field)
    both = lax.dot_general(
        jnp.concatenate([high, low], axis=0),
        high,
        (((1,), (1,)), ((), ())),
        preferred_element_type=jnp.float32,
    )
    cross = both[vectors:]
    gram = both[:vectors] + cross + cross.T
    half = vectors // 2
    first[mine] = jnp.concatenate([gram[:half], gram[half:]], axis=1)
    second[place] = exchange("vecs", mine, peers, first, s3, r3)
    total = exchange("cells", place, cells, second, s4, r4)
    gram = jnp.concatenate([total[:, :vectors], total[:, vectors:]], axis=0)
    frobenius = jnp.sqrt(jnp.sum(gram * gram, axis=(0, 1), keepdims=True))
    row = lax.broadcasted_iota(jnp.int32, gram.shape, 0)
    column = lax.broadcasted_iota(jnp.int32, gram.shape, 1)
    unit = jnp.where(row == column, 1.5, 0.0)
    mixing = (unit - 0.5 * gram / frobenius) / jnp.sqrt(frobenius)
    mixing_high, mixing_low = split_pair(mixing.T)
    result = factor * jnp.dot(
        jnp.concatenate([mixing_high, mixing_high, mixing_low], axis=1),
        jnp.concatenate([high, low, high], axis=0),
        preferred_element_type=jnp.float32,
    )
    for p in range(peers):
        for o in range(rows):
            mixed[p, o] = result[p * bundle : (p + 1) * bundle, o * lanes : (o + 1) * lanes]
    copies = []
    for turn in range(1, peers):
        p = lax.rem(mine + turn, peers)
        copies.append(remote(mixed.at[p], out_ref.at[mine], s5.at[turn], r5.at[turn], {"vecs": p}))
    for each in copies:
        each.start()
    out_ref[mine] = mixed[mine]
    for each in copies:
        each.wait()


def resident_shards(vectors, potential, hopping, center):
    orbits, _, bundle, lanes = vectors.shape
    cells, peers = lax.axis_size("cells"), lax.axis_size("vecs")
    own, rows, planes = bundle // cells, orbits // peers, cells
    count = bundle * peers
    vmem, smem = pl.BlockSpec(memory_space=pltpu.VMEM), pl.BlockSpec(memory_space=pltpu.SMEM)
    held = pl.BlockSpec(memory_space=pl.ANY)
    f32, bf16, dma = jnp.float32, jnp.bfloat16, pltpu.SemaphoreType.DMA
    sizes = [n for n in (cells, cells, cells * peers, peers, cells, peers) for _ in range(2)]
    result = pl.pallas_call(
        functools.partial(whole_kernel, cells, peers, math.sqrt(float(cells * lanes))),
        out_shape=jax.ShapeDtypeStruct((peers, rows, bundle, lanes), f32),
        in_specs=[smem, held, held, held],
        out_specs=vmem,
        scratch_shapes=[
            pltpu.VMEM((orbits * bundle, lanes), f32),
            pltpu.VMEM(potential.shape, f32),
            pltpu.VMEM(hopping.shape, f32),
            pltpu.VMEM((cells, own * orbits, lanes), f32),
            pltpu.VMEM((orbits, lanes), f32),
            pltpu.VMEM((cells, own * orbits, lanes), f32),
            pltpu.VMEM((cells, orbits, lanes), f32),
            pltpu.VMEM((9 * orbits, 9 * orbits), bf16),
            pltpu.VMEM((2, planes, orbits, own * lanes), f32),
            pltpu.VMEM((2, planes, orbits, own * lanes), bf16),
            pltpu.VMEM((2, planes, orbits, own * lanes), bf16),
            pltpu.VMEM((planes, peers, own * rows, lanes), f32),
            pltpu.VMEM((peers * planes, own * rows, lanes), f32),
            pltpu.VMEM((peers, count // 2, 2 * count), f32),
            pltpu.VMEM((cells, count // 2, 2 * count), f32),
            pltpu.VMEM((peers, rows, bundle, lanes), f32),
        ]
        + [dma((3,))]
        + [dma((n,)) for n in sizes],
        compiler_params=pltpu.CompilerParams(
            collective_id=0, has_side_effects=True, vmem_limit_bytes=62 * 1024 * 1024
        ),
        name="whole",
    )(center, vectors.reshape(orbits * bundle, lanes), potential, hopping)
    return result.reshape(orbits, 1, bundle, lanes)


def solution(mesh):
    placed = (P(None, "cells", "vecs", None), P(None, "cells", None), P(), P())

    def body(vectors, potential, hopping, center):
        _, width, bundle, merged = vectors.shape
        fits = (
            width == 1
            and bundle % lax.axis_size("cells") == 0
            and vectors.shape[0] % (8 * lax.axis_size("vecs")) == 0
            and merged == 128
        )
        return (resident_shards if fits else shards)(vectors, potential, hopping, center)

    return jax.shard_map(
        body,
        mesh=mesh,
        in_specs=placed,
        out_specs=P(None, "cells", "vecs", None),
        check_vma=False,
    )
```

```python
import functools
import math

import jax
import jax.numpy as jnp
from jax import lax
from jax.experimental import pallas as pl
from jax.experimental.pallas import tpu as pltpu
from jax.sharding import PartitionSpec as P

NVEC = 64
NY = 16
STEPS = 4
NZ = 8


HIGH = lax.Precision.HIGHEST


def with_halo(x, sides, width):
    for axis, dim in sides:
        peers, length = (lax.axis_size(axis), x.shape[dim])
        up = [(i, (i + 1) % peers) for i in range(peers)]
        down = [(j, i) for i, j in up]
        last = lax.slice_in_dim(x, length - width, length, axis=dim)
        initial = lax.slice_in_dim(x, 0, width, axis=dim)
        before = lax.ppermute(last, axis, up)
        after = lax.ppermute(initial, axis, down)
        x = jnp.concatenate([before, x, after], axis=dim)
    return x


def symmetric_blocks(hopping):
    return 0.5 * (hopping + jnp.transpose(hopping[::-1], (0, 2, 1)))


def apply_lattice(field_in, potential, center, blocks):
    orbits, width_x, bundle, merged = field_in.shape
    padded = with_halo(field_in, (("cells", 1),), 1)
    grid_view = padded.reshape(orbits, width_x + 2, bundle, NY, NZ)
    running = (potential - center[0])[:, :, None, :] * field_in
    for inner in range(9):
        shift_y = inner // 3 - 1
        shift_z = inner % 3 - 1
        shifted = jnp.roll(grid_view, (-shift_y, -shift_z), axis=(3, 4)).reshape(
            orbits, width_x + 2, bundle, merged
        )
        for offset in range(3):
            source = shifted[:, offset : offset + width_x].reshape(orbits, -1)
            product = jnp.dot(
                blocks[9 * offset + inner],
                source,
                precision=HIGH,
                preferred_element_type=jnp.float32,
            )
            running = running + product.reshape(orbits, width_x, bundle, merged)
    return running


def inner_rows(left, right):
    return lax.dot_general(
        left,
        right,
        (((0, 1, 3), (0, 1, 3)), ((), ())),
        precision=HIGH,
        preferred_element_type=jnp.float32,
    )


def shards(vectors, potential, hopping, center):
    blocks = symmetric_blocks(hopping)
    previous = vectors
    current = apply_lattice(vectors, potential, center, blocks)
    for step in range(STEPS - 1):
        following = 2.0 * apply_lattice(current, potential, center, blocks) - previous
        previous, current = (current, following)
    total_cells = current.shape[1] * lax.axis_size("cells") * current.shape[3]
    factor = math.sqrt(float(total_cells))
    by_cells = lax.all_to_all(current, "vecs", split_axis=3, concat_axis=2, tiled=True)
    gram_matrix = lax.psum(inner_rows(by_cells, by_cells), ("cells", "vecs"))
    frobenius = jnp.sqrt(jnp.sum(gram_matrix * gram_matrix))
    mixing = (1.5 * jnp.eye(NVEC, dtype=jnp.float32) - 0.5 * gram_matrix / frobenius) / jnp.sqrt(
        frobenius
    )
    mixed = jnp.einsum("oxuc,uv->oxvc", by_cells, mixing, precision=HIGH) * factor
    return lax.all_to_all(mixed, "vecs", split_axis=2, concat_axis=3, tiled=True)


def split_pair(value):
    high = value.astype(jnp.bfloat16)
    low = (value - high.astype(jnp.float32)).astype(jnp.bfloat16)
    return high, low


def build_weights(hopping_ref, weights):
    orbits = hopping_ref.shape[1]
    for inner in range(9):
        parts = []
        for offset in range(3):
            d = 9 * offset + inner
            parts.append(0.5 * (hopping_ref[d] + hopping_ref[26 - d].T))
        row = jnp.concatenate(parts, axis=1)
        high = row.astype(jnp.bfloat16).astype(jnp.float32)
        low = row - high
        weights[inner * orbits : (inner + 1) * orbits, :] = jnp.concatenate(
            [high, high, low], axis=1
        ).astype(jnp.bfloat16)


def gather_shifts(product, orbits):
    lanes = product.shape[1]
    z = lax.broadcasted_iota(jnp.int32, (orbits, lanes), 1) % NZ

    def part(dy, dz):
        if abs(dy) > 1:
            return 0.0
        at = (3 * (dy + 1) + dz + 1) * orbits
        return product[at : at + orbits]

    def moved(value, shift):
        shift = shift % lanes
        return pltpu.roll(value, shift, 1) if shift else value

    total = part(0, 0) + moved(part(-1, 0), NZ) + moved(part(1, 0), -NZ)
    for k in range(-2, 2):
        chosen = jnp.where(z > 0, part(k, 1), part(k + 1, 1))
        total = total + moved(chosen, -1 - NZ * k)
    for k in range(-1, 3):
        chosen = jnp.where(z < NZ - 1, part(k, -1), part(k - 1, -1))
        total = total + moved(chosen, 1 - NZ * k)
    return total


def remote(source, target, send, receive, device):
    return pltpu.make_async_remote_copy(
        src_ref=source,
        dst_ref=target,
        send_sem=send,
        recv_sem=receive,
        device_id=device,
        device_id_type=pl.DeviceIdType.MESH,
    )


def exchange(axis, me, count, slots, send_sems, recv_sems):
    copies = [
        remote(
            slots.at[me],
            slots.at[me],
            send_sems.at[hop],
            recv_sems.at[hop],
            {axis: lax.rem(me + hop, count)},
        )
        for hop in range(1, count)
    ]
    for each in copies:
        each.start()
    for each in copies:
        each.wait()
    total = slots[0]
    for i in range(1, count):
        total = total + slots[i]
    return total


def demand_order(planes):
    order, known = [], {(1, x) for x in range(planes)}

    def need(step, x):
        if (step, x) in known:
            return
        for near in (-1, 0, 1):
            need(step - 1, (x + near) % planes)
        known.add((step, x))
        order.append((step, x))

    for x in list(range(1, planes)) + [0]:
        need(STEPS, x)
    return order


def whole_kernel(
    cells, peers, factor,
    center_ref, vectors_any, potential_any, hopping_any, out_ref,
    vectors_ref, potential_ref, hopping_ref,
    packed, onsite_ref, planes_in, onsite_in, weights, fields, highs, lows, leaving, by_rows,
    first, second, mixed,
    local, s1, r1, s6, r6, s2, r2, s3, r3, s4, r4, s5, r5,
):
    mine, place = lax.axis_index("vecs"), lax.axis_index("cells")
    orbits, lanes = hopping_ref.shape[1], packed.shape[2]
    bundle = vectors_ref.shape[0] // orbits
    own, rows, planes = bundle // cells, orbits // peers, cells
    vectors = bundle * peers
    me = mine * cells + place

    loads = [
        pltpu.make_async_copy(source, target, local.at[n])
        for n, (source, target) in enumerate(
            (
                (vectors_any, vectors_ref),
                (potential_any, potential_ref),
                (hopping_any, hopping_ref),
            )
        )
    ]
    for each in loads:
        each.start()
    barrier = pltpu.get_barrier_semaphore()
    for hop in range(cells):
        for turn in range(peers):
            if hop or turn:
                pl.semaphore_signal(
                    barrier,
                    inc=1,
                    device_id={
                        "cells": lax.rem(place + hop, cells),
                        "vecs": lax.rem(mine + turn, peers),
                    },
                    device_id_type=pl.DeviceIdType.MESH,
                )

    loads[0].wait()
    for n in range(bundle):
        d, t = n // own, n % own
        packed[d, t * orbits : (t + 1) * orbits, :] = vectors_ref[pl.ds(n, orbits, stride=bundle), :]
    loads[1].wait()
    onsite = potential_ref[:, 0, :] - center_ref[0]
    onsite_ref[...] = onsite
    onsite_in[0] = onsite

    pl.semaphore_wait(barrier, cells * peers - 1)
    plane_copies, onsite_copies = [], []
    for hop in range(1, cells):
        peer, slot = lax.rem(place + hop, cells), cells - hop
        plane_copies.append(
            remote(packed.at[peer], planes_in.at[slot], s1.at[hop], r1.at[hop], {"cells": peer})
        )
        onsite_copies.append(
            remote(onsite_ref, onsite_in.at[slot], s6.at[hop], r6.at[hop], {"cells": peer})
        )
    for each in plane_copies + onsite_copies:
        each.start()
    loads[2].wait()
    build_weights(hopping_ref, weights)
    for each in plane_copies:
        each.wait()

    def put(slot, x, value):
        fields[slot, x] = value
        high, low = split_pair(value)
        highs[slot, x], lows[slot, x] = high, low

    for x in range(planes):
        held = packed.at[place] if x == 0 else planes_in.at[x]
        put(0, x, jnp.concatenate([held[t * orbits : (t + 1) * orbits, :] for t in range(own)], axis=1))

    def advance(step, x):
        now, later = (step - 1) % 2, step % 2
        around = [(x + near) % planes for near in (-1, 0, 1)]
        high, low = [highs[now, r] for r in around], [lows[now, r] for r in around]
        source = jnp.concatenate(high + low + high, axis=0)
        product = jnp.dot(weights[...], source, preferred_element_type=jnp.float32)
        moved = [gather_shifts(product[:, t * lanes : (t + 1) * lanes], orbits) for t in range(own)]
        if step == 1:
            return moved
        return [
            2.0 * (each + onsite_in[x] * fields[now, x, :, span]) - fields[later, x, :, span]
            for each, span in zip(moved, spans)
        ]

    spans = [slice(t * lanes, (t + 1) * lanes) for t in range(own)]
    for x in range(planes):
        fields[1, x] = jnp.concatenate(advance(1, x), axis=1)
    for each in onsite_copies:
        each.wait()
    for x in range(planes):
        onsite = jnp.concatenate([onsite_in[x]] * own, axis=1)
        put(1, x, fields[1, x] + onsite * fields[0, x])

    copies = []
    for step, x in demand_order(planes):
        results = advance(step, x)
        if step < STEPS:
            put(step % 2, x, jnp.concatenate(results, axis=1))
            continue
        for t in range(own):
            for p in range(peers):
                leaving[x, p, t * rows : (t + 1) * rows, :] = results[t][p * rows : (p + 1) * rows]
        for turn in list(range(1, peers)) + ([0] if x else []):
            p = lax.rem(mine + turn, peers)
            sem = x * peers + turn
            copy = remote(
                leaving.at[x, p],
                by_rows.at[me],
                s2.at[sem],
                r2.at[sem],
                {"cells": lax.rem(place + x, cells), "vecs": p},
            )
            copy.start()
            copies.append(copy)
    by_rows[me] = leaving[0, mine]
    for each in copies:
        each.wait()

    flat = by_rows.reshape(vectors * rows, lanes)
    field = jnp.concatenate(
        [flat[pl.ds(o, vectors, stride=rows), :] for o in range(rows)], axis=1
    )
    high, low = split_pair(field)
    both = lax.dot_general(
        jnp.concatenate([high, low], axis=0),
        high,
        (((1,), (1,)), ((), ())),
        preferred_element_type=jnp.float32,
    )
    cross = both[vectors:]
    gram = both[:vectors] + cross + cross.T
    half = vectors // 2
    first[mine] = jnp.concatenate([gram[:half], gram[half:]], axis=1)
    second[place] = exchange("vecs", mine, peers, first, s3, r3)
    total = exchange("cells", place, cells, second, s4, r4)
    gram = jnp.concatenate([total[:, :vectors], total[:, vectors:]], axis=0)
    frobenius = jnp.sqrt(jnp.sum(gram * gram, axis=(0, 1), keepdims=True))
    row = lax.broadcasted_iota(jnp.int32, gram.shape, 0)
    column = lax.broadcasted_iota(jnp.int32, gram.shape, 1)
    unit = jnp.where(row == column, 1.5, 0.0)
    mixing = (unit - 0.5 * gram / frobenius) / jnp.sqrt(frobenius)
    mixing_high, mixing_low = split_pair(mixing.T)
    result = factor * jnp.dot(
        jnp.concatenate([mixing_high, mixing_high, mixing_low], axis=1),
        jnp.concatenate([high, low, high], axis=0),
        preferred_element_type=jnp.float32,
    )
    for p in range(peers):
        for o in range(rows):
            mixed[p, o] = result[p * bundle : (p + 1) * bundle, o * lanes : (o + 1) * lanes]
    copies = []
    for turn in range(1, peers):
        p = lax.rem(mine + turn, peers)
        copies.append(remote(mixed.at[p], out_ref.at[mine], s5.at[turn], r5.at[turn], {"vecs": p}))
    for each in copies:
        each.start()
    out_ref[mine] = mixed[mine]
    for each in copies:
        each.wait()


def resident_shards(vectors, potential, hopping, center):
    orbits, _, bundle, lanes = vectors.shape
    cells, peers = lax.axis_size("cells"), lax.axis_size("vecs")
    own, rows, planes = bundle // cells, orbits // peers, cells
    count = bundle * peers
    vmem, smem = pl.BlockSpec(memory_space=pltpu.VMEM), pl.BlockSpec(memory_space=pltpu.SMEM)
    held = pl.BlockSpec(memory_space=pl.ANY)
    f32, bf16, dma = jnp.float32, jnp.bfloat16, pltpu.SemaphoreType.DMA
    sizes = [n for n in (cells, cells, cells * peers, peers, cells, peers) for _ in range(2)]
    result = pl.pallas_call(
        functools.partial(whole_kernel, cells, peers, math.sqrt(float(cells * lanes))),
        out_shape=jax.ShapeDtypeStruct((peers, rows, bundle, lanes), f32),
        in_specs=[smem, held, held, held],
        out_specs=vmem,
        scratch_shapes=[
            pltpu.VMEM((orbits * bundle, lanes), f32),
            pltpu.VMEM(potential.shape, f32),
            pltpu.VMEM(hopping.shape, f32),
            pltpu.VMEM((cells, own * orbits, lanes), f32),
            pltpu.VMEM((orbits, lanes), f32),
            pltpu.VMEM((cells, own * orbits, lanes), f32),
            pltpu.VMEM((cells, orbits, lanes), f32),
            pltpu.VMEM((9 * orbits, 9 * orbits), bf16),
            pltpu.VMEM((2, planes, orbits, own * lanes), f32),
            pltpu.VMEM((2, planes, orbits, own * lanes), bf16),
            pltpu.VMEM((2, planes, orbits, own * lanes), bf16),
            pltpu.VMEM((planes, peers, own * rows, lanes), f32),
            pltpu.VMEM((peers * planes, own * rows, lanes), f32),
            pltpu.VMEM((peers, count // 2, 2 * count), f32),
            pltpu.VMEM((cells, count // 2, 2 * count), f32),
            pltpu.VMEM((peers, rows, bundle, lanes), f32),
        ]
        + [dma((3,))]
        + [dma((n,)) for n in sizes],
        compiler_params=pltpu.CompilerParams(
            collective_id=0, has_side_effects=True, vmem_limit_bytes=62 * 1024 * 1024
        ),
        name="whole",
    )(center, vectors.reshape(orbits * bundle, lanes), potential, hopping)
    return result.reshape(orbits, 1, bundle, lanes)


def solution(mesh):
    placed = (P(None, "cells", "vecs", None), P(None, "cells", None), P(), P())

    def body(vectors, potential, hopping, center):
        _, width, bundle, merged = vectors.shape
        fits = (
            width == 1
            and bundle % lax.axis_size("cells") == 0
            and vectors.shape[0] % (8 * lax.axis_size("vecs")) == 0
            and merged == 128
        )
        return (resident_shards if fits else shards)(vectors, potential, hopping, center)

    return jax.shard_map(
        body,
        mesh=mesh,
        in_specs=placed,
        out_specs=P(None, "cells", "vecs", None),
        check_vma=False,
    )
```
